32 devices in a mesh: rows: 16 (over z, y, x), rep: 2 (over core).
Axes of the slice: x: 2, y: 2, z: 4, core: 2. Of those that a mesh axis runs over, the one named last changes fastest.
Arguments:
- features: bfloat16 [4096, 128], P('rows'), may hold values from -6 to 6
- node_order: int32 [4096], P('rows'), may hold values from 0 to 4095, as said below
- tile_vals: bfloat16 [6144, 128, 128], P(('rows', 'rep')), may hold values from -0.0546875 to 0.0546875
- tile_row: int32 [6144], P(('rows', 'rep')), may hold values from 0 to 31, as said below
- tile_col: int32 [6144], P(('rows', 'rep')), may hold values from 0 to 31, as said below
- tile_count: int32 [32], P(('rows', 'rep')), may hold values from 48 to 192, as said below
- weight: bfloat16 [128, 256], replicated, may hold values from -0.5 to 0.5
- bias: float32 [256], replicated, may hold values from -3 to 3
- cotangent: bfloat16 [4096, 256], P('rows'), may hold values from -6 to 6
Outputs:
- activations: bfloat16 [4096, 256], P('rows')
- weight_grad: float32 [128, 256], replicated
- bias_grad: float32 [256], replicated
The draws below stay inside these ranges and needn't reach their ends.
Inputs may be any that keep to these rules, and one draw needn't show every extreme that they name: `node_order`: positions c * 256 to c * 256 + 255 hold each of the node numbers c * 256 to c * 256 + 255 once. `tile_row`: slots d * 192 to d * 192 + 191 belong to device d = i * 2 + j (i along rows, j along rep); each of them names a row-block from i * 2 to i * 2 + 1. `tile_col`: A slot of device d = i * 2 + j names a column-block c * 2 + j + e for any node group c and any e from 0 to 0; slots may repeat a pair of row-block and column-block. Only the first tile_count[d] slots of device d are live; some device has exactly 192 and some other exactly 48.
All inputs are finite; a program needn't handle non-finite values.
Results may differ from the reference program's by a relative error of at most 0.0056.
Values may be sent and summed in bfloat16 or wider, within the bound.
A program may use at most 128 MiB of HBM per device.

```python
import jax
import jax.numpy as jnp
from jax import lax

F_IN = 128
HID = 256
BLOCK = 128
RB_DEV = 2
TILES_DEV = 192
REPLICAS = 2
NODES_DEV = 256
NB = 32
NODES = 4096
N_ROWS = 16
N_REP = 2
DEVICES = 32


def draw_node_order(key, part):
    group_count = NODES // NODES_DEV
    seg_keys = jax.random.split(jax.random.fold_in(key, 5), group_count)
    segments = jax.vmap(lambda single: jax.random.permutation(single, NODES_DEV))(seg_keys)
    offsets = (jnp.arange(group_count, dtype=jnp.int32) * NODES_DEV)[:, None]
    return (segments.astype(jnp.int32) + offsets).reshape(NODES)


def draw_tile_row(key, part):
    slot_total = DEVICES * TILES_DEV
    device = jnp.arange(slot_total, dtype=jnp.int32) // TILES_DEV
    row_group = device // REPLICAS
    choose = jax.random.randint(jax.random.fold_in(key, 3), (slot_total,), 0, RB_DEV, dtype=jnp.int32)
    return row_group * RB_DEV + choose


def draw_tile_col(key, part):
    slot_total = DEVICES * TILES_DEV
    device = jnp.arange(slot_total, dtype=jnp.int32) // TILES_DEV
    replica = device % REPLICAS
    half_blocks = RB_DEV // REPLICAS
    owner_key, within_key = jax.random.split(jax.random.fold_in(key, 7))
    owner = jax.random.randint(owner_key, (slot_total,), 0, DEVICES // REPLICAS, dtype=jnp.int32)
    within = jax.random.randint(within_key, (slot_total,), 0, half_blocks, dtype=jnp.int32)
    return owner * RB_DEV + replica * half_blocks + within


def draw_tile_count(key, part):
    first_key, second_key, third_key = jax.random.split(jax.random.fold_in(key, 11), 3)
    counts = jax.random.randint(first_key, (DEVICES,), TILES_DEV // 4, TILES_DEV + 1, dtype=jnp.int32)
    busiest = jax.random.randint(second_key, (), 0, DEVICES, dtype=jnp.int32)
    lightest = (busiest + jax.random.randint(third_key, (), 1, DEVICES, dtype=jnp.int32)) % DEVICES
    counts = counts.at[busiest].set(TILES_DEV)
    counts = counts.at[lightest].set(TILES_DEV // 4)
    return counts


def shard_levels(own_key, shape, cuts, low, largest):
    level = 1.0
    for position, shards_of in cuts:
        heights = jax.random.uniform(jax.random.fold_in(jax.random.fold_in(own_key, 6), position), (shards_of,), jnp.float32, low / len(cuts), largest / len(cuts))
        level = level * jnp.repeat(jnp.exp(heights), shape[position] // shards_of).reshape((-1,) + (1,) * (len(shape) - 1 - position))
    return level


def centred(rng, dims, spread, limit, cuts=(), kind=jnp.bfloat16):
    drawn = jax.random.normal(rng, dims, jnp.float32) * spread
    if len(cuts) > 0:
        drawn = shard_levels(rng, dims, cuts, -0.22, 0.18) * drawn
    return jnp.clip(drawn, min=-limit, max=limit).astype(kind)


def setup_inputs(seed: int = 0) -> dict:
    keys = jax.random.split(jax.random.key(seed), 10)
    return {
        "features": centred(keys[0], (NODES, F_IN), 1.0, 6.0, ((0, 16),)),
        "node_order": draw_node_order(jax.random.fold_in(keys[9], 71), 0),
        "tile_vals": centred(keys[2], (DEVICES * TILES_DEV, BLOCK, BLOCK), (BLOCK * TILES_DEV // RB_DEV) ** -0.5, 0.0546875, ((0, 32),)),
        "tile_row": draw_tile_row(jax.random.fold_in(keys[9], 71), 0),
        "tile_col": draw_tile_col(jax.random.fold_in(keys[9], 71), 0),
        "tile_count": draw_tile_count(jax.random.fold_in(keys[9], 71), 0),
        "weight": centred(keys[6], (F_IN, HID), F_IN ** -0.5, 0.5),
        "bias": centred(keys[7], (HID,), 0.5, 3.0, (), jnp.float32),
        "cotangent": centred(keys[8], (NODES, HID), 1.0, 6.0, ((0, 16),)),
    }


def silu_slope(pre_act):
    sigma = jax.nn.sigmoid(pre_act)
    return sigma * (1.0 + pre_act * (1.0 - sigma))


def reference(features, node_order, tile_vals, tile_row, tile_col, tile_count, weight, bias, cotangent):
    reordered = features[node_order]
    blocks = reordered.reshape(NB, BLOCK, F_IN)
    tile_stack = tile_vals.reshape(DEVICES, TILES_DEV, BLOCK, BLOCK)
    row_table = tile_row.reshape(DEVICES, TILES_DEV)
    col_table = tile_col.reshape(DEVICES, TILES_DEV)

    def one_device(packed):
        device, tile_set, row_ids, col_ids, tile_total = packed
        live_mask = (jnp.arange(TILES_DEV, dtype=jnp.int32) < tile_total).astype(jnp.float32)
        sources = blocks[col_ids].astype(jnp.float32)
        products = jnp.einsum("tij,tjf->tif", tile_set.astype(jnp.float32), sources, precision=lax.Precision.HIGHEST)
        owner_row = device // N_REP
        local_rows = row_ids - owner_row * RB_DEV
        select = (local_rows[:, None] == jnp.arange(RB_DEV, dtype=jnp.int32)[None, :]).astype(jnp.float32)
        select = select * live_mask[:, None]
        return jnp.einsum("tk,tif->kif", select, products, precision=lax.Precision.HIGHEST)

    partial_value = lax.map(one_device, (jnp.arange(DEVICES, dtype=jnp.int32), tile_stack, row_table, col_table, tile_count))
    summed = partial_value.reshape(N_ROWS, N_REP, NODES_DEV, F_IN).sum(axis=1)
    hidden = summed.reshape(NODES, F_IN).astype(jnp.bfloat16)
    pre_act = jnp.dot(hidden, weight, preferred_element_type=jnp.float32) + bias.astype(jnp.float32)
    activated = jax.nn.silu(pre_act).astype(jnp.bfloat16)
    activations = jnp.zeros((NODES, HID), jnp.bfloat16).at[node_order].set(activated)
    grad_reordered = cotangent[node_order].astype(jnp.float32)
    scaled = (grad_reordered * silu_slope(pre_act)).astype(jnp.bfloat16)
    grad_scale = float(NODES) ** -0.5
    weight_grad = lax.dot_general(hidden, scaled, (((0,), (0,)), ((), ())), preferred_element_type=jnp.float32) * grad_scale
    bias_grad = jnp.sum(scaled.astype(jnp.float32), axis=0) * grad_scale
    return activations, weight_grad, bias_grad
```

```python
import functools

import jax
import jax.numpy as jnp
from jax import lax
from jax.experimental import pallas as pl
from jax.experimental.pallas import tpu as pltpu
from jax.sharding import PartitionSpec as P

MESH = pl.DeviceIdType.MESH
SUBLANES = 8
CONTRACT_ROWS = (((0,), (0,)), ((), ()))


def kernel(
    n_rows, replicas, reducers, chunks, unroll,
    tile_row, tile_col, tile_count, order, features, weight, bias, cotangent, tiles_hbm,
    act_out, weight_out, bias_out,
    tiles, reordered, sources, grad_reordered, parts, terms, landed, finals,
    tile_sem, gather_send, gather_recv, part_send, part_recv, term_send, term_recv,
    final_send, final_recv,
):
    row = lax.axis_index("rows")
    replica = lax.axis_index("rep")
    slots, tile_size, _ = tiles.shape
    nodes, feat_width = features.shape
    hid = cotangent.shape[1]
    row_blocks = nodes // tile_size
    half_blocks = row_blocks // replicas
    zero_block = n_rows * half_blocks
    slice_rows = feat_width // reducers
    col_width = hid // replicas
    per_chunk = slots // chunks
    devices = n_rows * replicas

    def tile_copy(chunk):
        span = pl.ds(chunk * per_chunk, per_chunk)
        return pltpu.make_async_copy(tiles_hbm.at[span], tiles.at[span], tile_sem.at[chunk])

    for chunk in range(chunks):
        tile_copy(chunk).start()

    barrier = pltpu.get_barrier_semaphore()
    me = row * replicas + replica

    @pl.loop(1, devices)
    def _(off):
        other = lax.rem(me + off, devices)
        pl.semaphore_signal(
            barrier, inc=1, device_id=(other // replicas, lax.rem(other, replicas)),
            device_id_type=MESH,
        )

    local = order[...] - row * nodes
    place = (lax.broadcasted_iota(jnp.int32, (nodes, nodes), 0) == local).astype(jnp.bfloat16)
    mine = lax.dot_general(
        place, features[...], CONTRACT_ROWS, preferred_element_type=jnp.float32
    ).astype(jnp.bfloat16)
    reordered[...] = mine.reshape(row_blocks, tile_size, feat_width)
    sources[zero_block] = jnp.zeros((tile_size, feat_width), jnp.bfloat16)
    own_blocks = pl.ds(replica * half_blocks, half_blocks)
    sources[pl.ds(row * half_blocks, half_blocks)] = reordered[own_blocks]

    pl.semaphore_wait(barrier, devices - 1)

    def gather_copy(source, target):
        return pltpu.make_async_remote_copy(
            src_ref=reordered.at[own_blocks],
            dst_ref=sources.at[pl.ds(source * half_blocks, half_blocks)],
            send_sem=gather_send.at[target],
            recv_sem=gather_recv.at[source],
            device_id=(target, replica),
            device_id_type=MESH,
        )

    @pl.loop(1, n_rows)
    def _(off):
        gather_copy(row, lax.rem(row + off, n_rows)).start()

    grad_reordered[...] = lax.dot_general(
        place, cotangent[...], CONTRACT_ROWS, preferred_element_type=jnp.float32
    )

    for chunk in range(chunks):
        tile_copy(chunk).wait()

    @pl.loop(1, n_rows)
    def _(off):
        gather_copy(lax.rem(row + n_rows - off, n_rows), row).wait_recv()

    live = tile_count[0]
    first_block = row * row_blocks

    def aggregate(step, acc):
        left, right = [], []
        for sub in range(unroll):
            slot = step * unroll + sub
            col = tile_col[slot]
            position = (
                col // row_blocks * half_blocks + lax.rem(col, row_blocks) - replica * half_blocks
            )
            block = jnp.where(slot < live, tile_row[slot] - first_block, row_blocks)
            left.append(tiles[slot])
            right.append(
                jnp.concatenate(
                    [
                        sources[jnp.where(block == which, position, zero_block)]
                        for which in range(row_blocks)
                    ],
                    axis=1,
                )
            )
        return acc + jnp.dot(
            jnp.concatenate(left, axis=1),
            jnp.concatenate(right, axis=0),
            preferred_element_type=jnp.float32,
        )

    acc = lax.fori_loop(
        0, slots // unroll, aggregate, jnp.zeros((tile_size, row_blocks * feat_width), jnp.float32)
    )
    for which in range(row_blocks):
        parts[replica, which] = acc[:, which * feat_width:(which + 1) * feat_width]

    def part_copy(source, target):
        return pltpu.make_async_remote_copy(
            src_ref=parts.at[source],
            dst_ref=parts.at[source],
            send_sem=part_send.at[target],
            recv_sem=part_recv.at[source],
            device_id=(row, target),
            device_id_type=MESH,
        )

    for off in range(1, replicas):
        part_copy(replica, lax.rem(replica + off, replicas)).start()
    for off in range(1, replicas):
        part_copy(lax.rem(replica + replicas - off, replicas), replica).wait_recv()

    total = parts[0]
    for which in range(1, replicas):
        total = total + parts[which]
    hidden = total.reshape(nodes, feat_width).astype(jnp.bfloat16)
    pre_act = jnp.dot(hidden, weight[...], preferred_element_type=jnp.float32) + bias[...]
    sigma = 1.0 / (1.0 + jnp.exp(-pre_act))
    slope = sigma * (1.0 + pre_act * (1.0 - sigma))
    scaled = (grad_reordered[...] * slope).astype(jnp.bfloat16)
    weight_term = lax.dot_general(
        hidden, scaled, CONTRACT_ROWS, preferred_element_type=jnp.float32
    )
    bias_term = jnp.sum(scaled.astype(jnp.float32), axis=0, keepdims=True)
    pad = jnp.zeros((SUBLANES - replicas, col_width), jnp.float32)
    bias_rows = jnp.concatenate(
        [bias_term[:, j * col_width:(j + 1) * col_width] for j in range(replicas)] + [pad], axis=0
    )
    for j in range(replicas):
        terms[j, :, :slice_rows] = weight_term[:, j * col_width:(j + 1) * col_width].reshape(
            reducers, slice_rows, col_width
        )
        for k in range(reducers):
            terms[j, k, slice_rows:] = bias_rows

    def term_copy(source, target):
        return pltpu.make_async_remote_copy(
            src_ref=terms.at[replica, target],
            dst_ref=landed.at[source],
            send_sem=term_send.at[target],
            recv_sem=term_recv.at[source],
            device_id=(target, replica),
            device_id_type=MESH,
        )

    def final_copy(source, source_rep, target, target_rep):
        return pltpu.make_async_remote_copy(
            src_ref=finals.at[source, source_rep],
            dst_ref=finals.at[source, source_rep],
            send_sem=final_send.at[target, target_rep],
            recv_sem=final_recv.at[source, source_rep],
            device_id=(target, target_rep),
            device_id_type=MESH,
        )

    def for_reducers(action):
        @pl.loop(0, reducers)
        def _(k):
            @pl.when(k != row)
            def _():
                action(k)

    for_reducers(lambda k: term_copy(row, k).start())

    activated = (pre_act * sigma).astype(jnp.bfloat16)
    act_out[...] = jnp.dot(place, activated, preferred_element_type=jnp.float32).astype(
        jnp.bfloat16
    )

    def reduce_slice():
        landed[row] = terms[replica, row]

        @pl.loop(1, n_rows)
        def _(off):
            term_copy(lax.rem(row + n_rows - off, n_rows), row).wait_recv()

        summed = landed[0]
        for k in range(1, n_rows):
            summed = summed + landed[k]
        finals[row, replica] = summed * float(nodes * n_rows) ** (-0.5)

        @pl.loop(1, devices)
        def _(off):
            other = lax.rem(me + off, devices)
            final_copy(row, replica, other // replicas, lax.rem(other, replicas)).start()

    if reducers == n_rows:
        reduce_slice()
    else:
        pl.when(row < reducers)(reduce_slice)

    def for_finals(action):
        @pl.loop(0, reducers * replicas)
        def _(k):
            @pl.when(k != me)
            def _():
                action(k // replicas, lax.rem(k, replicas))

    for_finals(lambda k, j: final_copy(k, j, row, replica).wait_recv())
    for j in range(replicas):
        weight_out[:, j * col_width:(j + 1) * col_width] = finals[:, j, :slice_rows].reshape(
            feat_width, col_width
        )
        bias_out[:, j * col_width:(j + 1) * col_width] = finals[0, 0, slice_rows + j:slice_rows + j + 1]

    @pl.loop(1, n_rows)
    def _(off):
        gather_copy(row, lax.rem(row + off, n_rows)).wait_send()

    for off in range(1, replicas):
        part_copy(replica, lax.rem(replica + off, replicas)).wait_send()
    for_reducers(lambda k: term_copy(row, k).wait_send())

    def drain():
        @pl.loop(1, devices)
        def _(off):
            other = lax.rem(me + off, devices)
            final_copy(row, replica, other // replicas, lax.rem(other, replicas)).wait_send()

    if reducers == n_rows:
        drain()
    else:
        pl.when(row < reducers)(drain)


def body(n_rows, replicas, features, node_order, tile_vals, tile_row, tile_col, tile_count, weight, bias, cotangent):
    nodes, feat_width = features.shape
    hid = cotangent.shape[1]
    slots, tile_size, _ = tile_vals.shape
    row_blocks = nodes // tile_size
    half_blocks = row_blocks // replicas
    reducers = min(n_rows, feat_width // SUBLANES)
    slice_rows = feat_width // reducers
    payload = slice_rows + SUBLANES
    col_width = hid // replicas
    chunks = 4
    vmem = pl.BlockSpec(memory_space=pltpu.VMEM)
    smem = pl.BlockSpec(memory_space=pltpu.SMEM)
    dma = pltpu.SemaphoreType.DMA
    activations, weight_grad, bias_grad = pl.pallas_call(
        functools.partial(kernel, n_rows, replicas, reducers, chunks, 8),
        out_shape=(
            jax.ShapeDtypeStruct((nodes, hid), jnp.bfloat16),
            jax.ShapeDtypeStruct((feat_width, hid), jnp.float32),
            jax.ShapeDtypeStruct((1, hid), jnp.float32),
        ),
        in_specs=[smem] * 3 + [vmem] * 5 + [pl.BlockSpec(memory_space=pl.ANY)],
        out_specs=(vmem, vmem, vmem),
        scratch_shapes=[
            pltpu.VMEM((slots, tile_size, tile_size), jnp.bfloat16),
            pltpu.VMEM((row_blocks, tile_size, feat_width), jnp.bfloat16),
            pltpu.VMEM((n_rows * half_blocks + 1, tile_size, feat_width), jnp.bfloat16),
            pltpu.VMEM((nodes, hid), jnp.float32),
            pltpu.VMEM((replicas, row_blocks, tile_size, feat_width), jnp.float32),
            pltpu.VMEM((replicas, reducers, payload, col_width), jnp.float32),
            pltpu.VMEM((n_rows, payload, col_width), jnp.float32),
            pltpu.VMEM((reducers, replicas, payload, col_width), jnp.float32),
            dma((chunks,)),
            dma((n_rows,)),
            dma((n_rows,)),
            dma((replicas,)),
            dma((replicas,)),
            dma((reducers,)),
            dma((n_rows,)),
            dma((n_rows, replicas)),
            dma((reducers, replicas)),
        ],
        compiler_params=pltpu.CompilerParams(
            collective_id=0, has_side_effects=True, vmem_limit_bytes=48 * 1024 * 1024
        ),
    )(
        tile_row, tile_col, tile_count, node_order.reshape(1, nodes), features, weight,
        bias.reshape(1, hid), cotangent, tile_vals,
    )
    return activations, weight_grad, bias_grad.reshape(hid)


def solution(mesh):
    return jax.shard_map(
        functools.partial(body, mesh.shape["rows"], mesh.shape["rep"]),
        mesh=mesh,
        in_specs=(
            P("rows", None),
            P("rows"),
            P(("rows", "rep"), None, None),
            P(("rows", "rep")),
            P(("rows", "rep")),
            P(("rows", "rep")),
            P(),
            P(),
            P("rows", None),
        ),
        out_specs=(P("rows", None), P(), P()),
        check_vma=False,
    )
```

```python
import functools
import math

import jax
import jax.numpy as jnp
from jax import lax
from jax.experimental import pallas as pl
from jax.experimental.pallas import tpu as pltpu
from jax.sharding import PartitionSpec as P

MESH = pl.DeviceIdType.MESH
BIAS_ROWS = 16
CONTRACT_ROWS = (((0,), (0,)), ((), ()))


def kernel(
    n_rows, replicas, plane, chunks, unroll,
    tile_row_hbm, tile_col_hbm, tile_count_hbm, order_hbm, features_hbm, weight_hbm, bias_hbm,
    cotangent_hbm, tiles_hbm,
    act_out, weight_out, bias_out,
    tile_row, tile_col, tile_count, order, features, weight, bias, cotangent, activated, input_sem,
    act_sem, tiles, sources, grad_reordered, parts, terms, finals,
    tile_sem, gather_column, gather_plane, gather_recv, part_send, part_recv,
    term_column, term_plane, term_recv, final_send, final_recv,
):
    row = lax.axis_index("rows")
    replica = lax.axis_index("rep")
    slots, tile_size, _ = tiles.shape
    nodes, feat_width = features.shape
    hid = cotangent.shape[1]
    row_blocks = nodes // tile_size
    half_blocks = row_blocks // replicas
    zero_block = n_rows * half_blocks
    col_width = hid // replicas
    per_chunk = slots // chunks
    depth = n_rows // plane
    layer = row // plane
    spot = lax.rem(row, plane)
    toward = 1 - 2 * (layer // ((depth + 1) // 2))

    def column_peer(off):
        return lax.rem(layer + toward * off + depth, depth) * plane + spot

    def plane_peer(off):
        return layer * plane + lax.rem(spot + off, plane)

    inputs = [
        pltpu.make_async_copy(source, target, input_sem.at[k])
        for k, (source, target) in enumerate([
            (order_hbm, order), (features_hbm, features), (cotangent_hbm, cotangent),
            (tile_row_hbm, tile_row), (tile_col_hbm, tile_col), (tile_count_hbm, tile_count),
            (weight_hbm, weight), (bias_hbm, bias),
        ])
    ]
    for copy in inputs:
        copy.start()

    def tile_copy(chunk):
        span = pl.ds(chunk * per_chunk, per_chunk)
        return pltpu.make_async_copy(tiles_hbm.at[span], tiles.at[span], tile_sem.at[chunk])

    for chunk in range(chunks):
        tile_copy(chunk).start()

    barrier = pltpu.get_barrier_semaphore()

    def greet(target, target_rep):
        pl.semaphore_signal(
            barrier, inc=1, device_id=(target, target_rep), device_id_type=MESH
        )

    @pl.loop(1, depth)
    def _(off):
        greet(column_peer(off), replica)

    for off in range(1, plane):
        greet(plane_peer(off), replica)
    for off in range(1, replicas):
        greet(row, lax.rem(replica + off, replicas))

    class Spread:
        def __init__(self, view, column_sem, plane_sem, recv_sem):
            self.view, self.recv_sem = view, recv_sem
            self.column_sem, self.plane_sem = column_sem, plane_sem

        def copy(self, block, target, send_sem):
            return pltpu.make_async_remote_copy(
                src_ref=self.view(block),
                dst_ref=self.view(block),
                send_sem=send_sem,
                recv_sem=self.recv_sem.at[block],
                device_id=(target, replica),
                device_id_type=MESH,
            )

        def along_column(self, off):
            return self.copy(row, column_peer(off), self.column_sem.at[off])

        def through_plane(self, step, off):
            block = row if step is None else column_peer(step)
            step = 0 if step is None else step
            return self.copy(block, plane_peer(off), self.plane_sem.at[step, off])

        def start(self):
            @pl.loop(1, depth)
            def _(off):
                self.along_column(depth - off).start()

            for off in range(1, plane):
                self.through_plane(None, off).start()

        def relay(self):
            @pl.loop(1, depth)
            def _(step):
                self.copy(column_peer(step), row, self.column_sem.at[0]).wait_recv()
                for off in range(1, plane):
                    self.through_plane(step, off).start()

        def finish(self):
            for off in range(1, plane):
                beside = lax.rem(spot + off, plane)

                @pl.loop(0, depth)
                def _(level):
                    self.copy(level * plane + beside, row, self.column_sem.at[0]).wait_recv()

        def drain(self):
            @pl.loop(1, depth)
            def _(off):
                self.along_column(off).wait_send()
                for beside in range(1, plane):
                    self.through_plane(off, beside).wait_send()

            for off in range(1, plane):
                self.through_plane(None, off).wait_send()

    def source_view(block):
        return sources.at[pl.ds(block * half_blocks, half_blocks)]

    gather = Spread(source_view, gather_column, gather_plane, gather_recv)
    reduction = Spread(lambda block: terms.at[block], term_column, term_plane, term_recv)

    inputs[0].wait()
    inputs[1].wait()
    local = order[...] - row * nodes
    place = (lax.broadcasted_iota(jnp.int32, (nodes, nodes), 0) == local).astype(jnp.bfloat16)
    mine = lax.dot_general(
        place, features[...], CONTRACT_ROWS, preferred_element_type=jnp.float32
    ).astype(jnp.bfloat16).reshape(replicas, half_blocks, tile_size, feat_width)
    own = mine[0]
    for which in range(1, replicas):
        own = jnp.where(replica == which, mine[which], own)
    sources[pl.ds(row * half_blocks, half_blocks)] = own
    sources[zero_block] = jnp.zeros((tile_size, feat_width), jnp.bfloat16)

    pl.semaphore_wait(barrier, depth - 1 + plane - 1 + replicas - 1)
    gather.start()

    inputs[2].wait()
    grad_reordered[...] = lax.dot_general(
        place, cotangent[...], CONTRACT_ROWS, preferred_element_type=jnp.float32
    )

    gather.relay()

    for copy in inputs[3:]:
        copy.wait()
    for chunk in range(chunks):
        tile_copy(chunk).wait()

    gather.finish()

    live = tile_count[0, 0]
    first_block = row * row_blocks

    def aggregate(step, acc):
        left, right = [], []
        for sub in range(unroll):
            slot = step * unroll + sub
            col = tile_col[slot]
            position = lax.div(col, row_blocks)
            if half_blocks > 1:
                position = position * half_blocks + lax.rem(col, half_blocks)
            block = jnp.where(slot < live, tile_row[slot] - first_block, row_blocks)
            left.append(tiles[slot])
            right.append(
                jnp.concatenate(
                    [
                        sources[jnp.where(block == which, position, zero_block)]
                        for which in range(row_blocks)
                    ],
                    axis=1,
                )
            )
        return acc + jnp.dot(
            jnp.concatenate(left, axis=1),
            jnp.concatenate(right, axis=0),
            preferred_element_type=jnp.float32,
        )

    acc = lax.fori_loop(
        0, slots // unroll, aggregate, jnp.zeros((tile_size, row_blocks * feat_width), jnp.float32)
    )
    for which in range(row_blocks):
        parts[replica, which] = acc[:, which * feat_width:(which + 1) * feat_width]

    def part_copy(source, target):
        return pltpu.make_async_remote_copy(
            src_ref=parts.at[source],
            dst_ref=parts.at[source],
            send_sem=part_send.at[target],
            recv_sem=part_recv.at[source],
            device_id=(row, target),
            device_id_type=MESH,
        )

    for off in range(1, replicas):
        part_copy(replica, lax.rem(replica + off, replicas)).start()
    for off in range(1, replicas):
        part_copy(lax.rem(replica + replicas - off, replicas), replica).wait_recv()

    total = parts[0]
    for which in range(1, replicas):
        total = total + parts[which]
    hidden = total.reshape(nodes, feat_width).astype(jnp.bfloat16)
    pre_act = jnp.dot(hidden, weight[...], preferred_element_type=jnp.float32) + bias[...]
    sigma = 1.0 / (1.0 + jnp.exp(-pre_act))
    slope = sigma * (1.0 + pre_act * (1.0 - sigma))
    scaled = (grad_reordered[...] * slope).astype(jnp.bfloat16)
    weight_term = lax.dot_general(
        hidden, scaled, CONTRACT_ROWS, preferred_element_type=jnp.float32
    )
    own_term = weight_term[:, :col_width]
    for which in range(1, replicas):
        own_term = jnp.where(
            replica == which, weight_term[:, which * col_width:(which + 1) * col_width], own_term
        )
    bias_term = jnp.sum(scaled.astype(jnp.float32), axis=0, keepdims=True)
    bias_high = bias_term.astype(jnp.bfloat16).astype(jnp.float32)
    bias_rows = [
        part[:, j * col_width:(j + 1) * col_width]
        for part in (bias_high, bias_term - bias_high)
        for j in range(replicas)
    ]
    pad = jnp.zeros((BIAS_ROWS - 2 * replicas, col_width), jnp.float32)
    terms[row, :feat_width] = own_term.astype(jnp.bfloat16)
    terms[row, feat_width:] = jnp.concatenate(bias_rows + [pad], axis=0).astype(jnp.bfloat16)
    reduction.start()

    activated[...] = jnp.dot(
        place, (pre_act * sigma).astype(jnp.bfloat16), preferred_element_type=jnp.float32
    ).astype(jnp.bfloat16)
    act_copy = pltpu.make_async_copy(activated, act_out, act_sem)
    act_copy.start()

    reduction.relay()
    reduction.finish()

    summed = terms[0].astype(jnp.float32)
    for k in range(1, n_rows):
        summed = summed + terms[k].astype(jnp.float32)
    summed = summed * float(nodes * n_rows) ** (-0.5)
    finals[replica] = summed[:feat_width]

    def final_copy(source, target):
        return pltpu.make_async_remote_copy(
            src_ref=finals.at[source],
            dst_ref=finals.at[source],
            send_sem=final_send.at[target],
            recv_sem=final_recv.at[source],
            device_id=(row, target),
            device_id_type=MESH,
        )

    for off in range(1, replicas):
        final_copy(replica, lax.rem(replica + off, replicas)).start()
    for j in range(replicas):
        high, low = feat_width + j, feat_width + replicas + j
        bias_out[:, j * col_width:(j + 1) * col_width] = (
            summed[high:high + 1] + summed[low:low + 1]
        )
    gather.drain()
    reduction.drain()
    for off in range(1, replicas):
        part_copy(replica, lax.rem(replica + off, replicas)).wait_send()
    act_copy.wait()
    for off in range(1, replicas):
        final_copy(lax.rem(replica + replicas - off, replicas), replica).wait_recv()
    for j in range(replicas):
        weight_out[:, j * col_width:(j + 1) * col_width] = finals[j]
    for off in range(1, replicas):
        final_copy(replica, lax.rem(replica + off, replicas)).wait_send()


def publish(act_in, weight_in, bias_in, act_out, weight_out, bias_out, sem):
    copies = [
        pltpu.make_async_copy(source, target, sem.at[k])
        for k, (source, target) in enumerate(
            [(act_in, act_out), (weight_in, weight_out), (bias_in, bias_out)]
        )
    ]
    for copy in copies:
        copy.start()
    for copy in copies:
        copy.wait()


def body(n_rows, replicas, features, node_order, tile_vals, tile_row, tile_col, tile_count, weight, bias, cotangent):
    nodes, feat_width = features.shape
    hid = cotangent.shape[1]
    slots, tile_size, _ = tile_vals.shape
    row_blocks = nodes // tile_size
    half_blocks = row_blocks // replicas
    col_width = hid // replicas
    plane = math.gcd(n_rows, 4)
    depth = n_rows // plane
    chunks = 4
    vmem = pl.BlockSpec(memory_space=pltpu.VMEM)
    dma = pltpu.SemaphoreType.DMA
    activations, weight_grad, bias_grad = pl.pallas_call(
        functools.partial(kernel, n_rows, replicas, plane, chunks, 24),
        out_shape=(
            jax.ShapeDtypeStruct((nodes, hid), jnp.bfloat16),
            jax.ShapeDtypeStruct((feat_width, hid), jnp.float32),
            jax.ShapeDtypeStruct((1, hid), jnp.float32),
        ),
        in_specs=[pl.BlockSpec(memory_space=pltpu.HBM)] * 9,
        out_specs=(pl.BlockSpec(memory_space=pltpu.HBM), vmem, vmem),
        scratch_shapes=[
            pltpu.SMEM(tile_row.shape, jnp.int32),
            pltpu.SMEM(tile_col.shape, jnp.int32),
            pltpu.SMEM((1, 1), jnp.int32),
            pltpu.VMEM((1, nodes), jnp.int32),
            pltpu.VMEM(features.shape, features.dtype),
            pltpu.VMEM(weight.shape, weight.dtype),
            pltpu.VMEM((1, hid), jnp.float32),
            pltpu.VMEM(cotangent.shape, cotangent.dtype),
            pltpu.VMEM((nodes, hid), jnp.bfloat16),
            dma((8,)),
            dma(()),
            pltpu.VMEM((slots, tile_size, tile_size), jnp.bfloat16),
            pltpu.VMEM((n_rows * half_blocks + 1, tile_size, feat_width), jnp.bfloat16),
            pltpu.VMEM((nodes, hid), jnp.float32),
            pltpu.VMEM((replicas, row_blocks, tile_size, feat_width), jnp.float32),
            pltpu.VMEM((n_rows, feat_width + BIAS_ROWS, col_width), jnp.bfloat16),
            pltpu.VMEM((replicas, feat_width, col_width), jnp.float32),
            dma((chunks,)),
            dma((depth,)),
            dma((depth, plane)),
            dma((n_rows,)),
            dma((replicas,)),
            dma((replicas,)),
            dma((depth,)),
            dma((depth, plane)),
            dma((n_rows,)),
            dma((replicas,)),
            dma((replicas,)),
        ],
        compiler_params=pltpu.CompilerParams(
            collective_id=0, has_side_effects=True, vmem_limit_bytes=67043328
        ),
    )(*(
        operand
        for operand in (
            tile_row, tile_col, tile_count.reshape(1, 1), node_order.reshape(1, nodes), features, weight,
            bias.reshape(1, hid), cotangent, tile_vals,
        )
    ))
    activations, weight_grad, bias_grad = pl.pallas_call(
        publish,
        out_shape=tuple(
            jax.ShapeDtypeStruct(part.shape, part.dtype)
            for part in (activations, weight_grad, bias_grad)
        ),
        in_specs=[vmem] * 3,
        out_specs=(pl.BlockSpec(memory_space=pltpu.HBM),) * 3,
        scratch_shapes=[dma((3,))],
    )(activations, weight_grad, bias_grad)
    return activations, weight_grad, bias_grad.reshape(hid)


def solution(mesh):
    return jax.shard_map(
        functools.partial(body, mesh.shape["rows"], mesh.shape["rep"]),
        mesh=mesh,
        in_specs=(
            P("rows", None),
            P("rows"),
            P(("rows", "rep"), None, None),
            P(("rows", "rep")),
            P(("rows", "rep")),
            P(("rows", "rep")),
            P(),
            P(),
            P("rows", None),
        ),
        out_specs=(P("rows", None), P(), P()),
        check_vma=False,
    )
```

```python
import functools
import math

import jax
import jax.numpy as jnp
from jax import lax
from jax.experimental import pallas as pl
from jax.experimental.pallas import tpu as pltpu
from jax.sharding import PartitionSpec as P

MESH = pl.DeviceIdType.MESH
BIAS_ROWS = 16
CONTRACT_ROWS = (((0,), (0,)), ((), ()))


def kernel(
    n_rows, replicas, plane, chunks, unroll,
    tile_row_hbm, tile_col_hbm, tile_count_hbm, order_hbm, features_hbm, weight_hbm, bias_hbm,
    cotangent_hbm, tiles_hbm,
    act_out, weight_out, bias_out,
    tile_row, tile_col, tile_count, order, features, weight, bias, cotangent, activated, input_sem,
    act_sem, tiles, sources, grad_reordered, parts, terms, sums, finals,
    tile_sem, gather_column, gather_plane, gather_recv, part_send, part_recv,
    term_send, term_recv, sum_send, sum_recv, final_send, final_recv,
):
    row = lax.axis_index("rows")
    replica = lax.axis_index("rep")
    slots, tile_size, _ = tiles.shape
    nodes, feat_width = features.shape
    hid = cotangent.shape[1]
    row_blocks = nodes // tile_size
    half_blocks = row_blocks // replicas
    zero_block = n_rows * half_blocks
    col_width = hid // replicas
    per_chunk = slots // chunks
    depth = n_rows // plane
    layer = row // plane
    spot = lax.rem(row, plane)
    toward = 1 - 2 * (layer // ((depth + 1) // 2))

    def column_peer(off):
        return lax.rem(layer + toward * off + depth, depth) * plane + spot

    def plane_peer(off):
        return layer * plane + lax.rem(spot + off, plane)

    inputs = [
        pltpu.make_async_copy(source, target, input_sem.at[k])
        for k, (source, target) in enumerate([
            (order_hbm, order), (features_hbm, features), (cotangent_hbm, cotangent),
            (tile_row_hbm, tile_row), (tile_col_hbm, tile_col), (tile_count_hbm, tile_count),
            (weight_hbm, weight), (bias_hbm, bias),
        ])
    ]
    for copy in inputs:
        copy.start()

    def tile_copy(chunk):
        span = pl.ds(chunk * per_chunk, per_chunk)
        return pltpu.make_async_copy(tiles_hbm.at[span], tiles.at[span], tile_sem.at[chunk])

    for chunk in range(chunks):
        tile_copy(chunk).start()

    barrier = pltpu.get_barrier_semaphore()

    def greet(target, target_rep):
        pl.semaphore_signal(
            barrier, inc=1, device_id=(target, target_rep), device_id_type=MESH
        )

    @pl.loop(1, depth)
    def _(off):
        greet(column_peer(off), replica)

    for off in range(1, plane):
        greet(plane_peer(off), replica)
    for off in range(1, replicas):
        greet(row, lax.rem(replica + off, replicas))

    class Spread:
        def __init__(self, view, column_sem, plane_sem, recv_sem):
            self.view, self.recv_sem = view, recv_sem
            self.column_sem, self.plane_sem = column_sem, plane_sem

        def copy(self, block, target, send_sem):
            return pltpu.make_async_remote_copy(
                src_ref=self.view(block),
                dst_ref=self.view(block),
                send_sem=send_sem,
                recv_sem=self.recv_sem.at[block],
                device_id=(target, replica),
                device_id_type=MESH,
            )

        def along_column(self, off):
            return self.copy(row, column_peer(off), self.column_sem.at[off])

        def through_plane(self, step, off):
            block = row if step is None else column_peer(step)
            step = 0 if step is None else step
            return self.copy(block, plane_peer(off), self.plane_sem.at[step, off])

        def start(self):
            @pl.loop(1, depth)
            def _(off):
                self.along_column(depth - off).start()

            for off in range(1, plane):
                self.through_plane(None, off).start()

        def relay(self):
            @pl.loop(1, depth)
            def _(step):
                self.copy(column_peer(step), row, self.column_sem.at[0]).wait_recv()
                for off in range(1, plane):
                    self.through_plane(step, off).start()

        def finish(self):
            for off in range(1, plane):
                beside = lax.rem(spot + off, plane)

                @pl.loop(0, depth)
                def _(level):
                    self.copy(level * plane + beside, row, self.column_sem.at[0]).wait_recv()

        def drain(self):
            @pl.loop(1, depth)
            def _(off):
                self.along_column(off).wait_send()
                for beside in range(1, plane):
                    self.through_plane(off, beside).wait_send()

            for off in range(1, plane):
                self.through_plane(None, off).wait_send()

    def source_view(block):
        return sources.at[pl.ds(block * half_blocks, half_blocks)]

    gather = Spread(source_view, gather_column, gather_plane, gather_recv)

    inputs[0].wait()
    inputs[1].wait()
    local = order[...] - row * nodes
    place = (lax.broadcasted_iota(jnp.int32, (nodes, nodes), 0) == local).astype(jnp.bfloat16)
    mine = lax.dot_general(
        place, features[...], CONTRACT_ROWS, preferred_element_type=jnp.float32
    ).astype(jnp.bfloat16).reshape(replicas, half_blocks, tile_size, feat_width)
    own = mine[0]
    for which in range(1, replicas):
        own = jnp.where(replica == which, mine[which], own)
    sources[pl.ds(row * half_blocks, half_blocks)] = own
    sources[zero_block] = jnp.zeros((tile_size, feat_width), jnp.bfloat16)

    pl.semaphore_wait(barrier, depth - 1 + plane - 1 + replicas - 1)
    gather.start()

    inputs[2].wait()
    grad_reordered[...] = lax.dot_general(
        place, cotangent[...], CONTRACT_ROWS, preferred_element_type=jnp.float32
    )

    gather.relay()

    for copy in inputs[3:]:
        copy.wait()
    for chunk in range(chunks):
        tile_copy(chunk).wait()

    gather.finish()

    live = tile_count[0, 0]
    first_block = row * row_blocks

    def aggregate(step, acc):
        left, right = [], []
        for sub in range(unroll):
            slot = step * unroll + sub
            col = tile_col[slot]
            position = lax.div(col, row_blocks)
            if half_blocks > 1:
                position = position * half_blocks + lax.rem(col, half_blocks)
            block = jnp.where(slot < live, tile_row[slot] - first_block, row_blocks)
            left.append(tiles[slot])
            right.append(
                jnp.concatenate(
                    [
                        sources[jnp.where(block == which, position, zero_block)]
                        for which in range(row_blocks)
                    ],
                    axis=1,
                )
            )
        return acc + jnp.dot(
            jnp.concatenate(left, axis=1),
            jnp.concatenate(right, axis=0),
            preferred_element_type=jnp.float32,
        )

    acc = lax.fori_loop(
        0, slots // unroll, aggregate, jnp.zeros((tile_size, row_blocks * feat_width), jnp.float32)
    )
    for which in range(row_blocks):
        parts[replica, which] = acc[:, which * feat_width:(which + 1) * feat_width]

    def part_copy(source, target):
        return pltpu.make_async_remote_copy(
            src_ref=parts.at[source],
            dst_ref=parts.at[source],
            send_sem=part_send.at[target],
            recv_sem=part_recv.at[source],
            device_id=(row, target),
            device_id_type=MESH,
        )

    for off in range(1, replicas):
        part_copy(replica, lax.rem(replica + off, replicas)).start()
    for off in range(1, replicas):
        part_copy(lax.rem(replica + replicas - off, replicas), replica).wait_recv()

    total = parts[0]
    for which in range(1, replicas):
        total = total + parts[which]
    hidden = total.reshape(nodes, feat_width).astype(jnp.bfloat16)
    pre_act = jnp.dot(hidden, weight[...], preferred_element_type=jnp.float32) + bias[...]
    sigma = 1.0 / (1.0 + jnp.exp(-pre_act))
    slope = sigma * (1.0 + pre_act * (1.0 - sigma))
    scaled = (grad_reordered[...] * slope).astype(jnp.bfloat16)
    weight_term = lax.dot_general(
        hidden, scaled, CONTRACT_ROWS, preferred_element_type=jnp.float32
    )
    own_term = weight_term[:, :col_width]
    for which in range(1, replicas):
        own_term = jnp.where(
            replica == which, weight_term[:, which * col_width:(which + 1) * col_width], own_term
        )
    bias_term = jnp.sum(scaled.astype(jnp.float32), axis=0, keepdims=True)
    bias_term = jnp.concatenate(
        [bias_term[:, j * col_width:(j + 1) * col_width] for j in range(replicas)], axis=0
    )

    def pack(target, term, bias_part):
        high = bias_part.astype(jnp.bfloat16).astype(jnp.float32)
        pad = jnp.zeros((BIAS_ROWS - 2 * replicas, col_width), jnp.float32)
        target[:feat_width] = term.astype(jnp.bfloat16)
        target[feat_width:] = jnp.concatenate([high, bias_part - high, pad], axis=0).astype(
            jnp.bfloat16
        )

    def unpack(held):
        summed = held[0].astype(jnp.float32)
        for k in range(1, held.shape[0]):
            summed = summed + held[k].astype(jnp.float32)
        low = feat_width + replicas
        return summed[:feat_width], summed[feat_width:low] + summed[low:low + replicas]

    def term_copy(source, off):
        return pltpu.make_async_remote_copy(
            src_ref=terms.at[source],
            dst_ref=terms.at[source],
            send_sem=term_send.at[off],
            recv_sem=term_recv.at[source],
            device_id=(column_peer(off), replica),
            device_id_type=MESH,
        )

    def sum_copy(source, off):
        return pltpu.make_async_remote_copy(
            src_ref=sums.at[source],
            dst_ref=sums.at[source],
            send_sem=sum_send.at[off],
            recv_sem=sum_recv.at[source],
            device_id=(plane_peer(off), replica),
            device_id_type=MESH,
        )

    pack(terms.at[layer], own_term, bias_term)

    @pl.loop(1, depth)
    def _(off):
        term_copy(layer, depth - off).start()

    activated[...] = jnp.dot(
        place, (pre_act * sigma).astype(jnp.bfloat16), preferred_element_type=jnp.float32
    ).astype(jnp.bfloat16)
    act_copy = pltpu.make_async_copy(activated, act_out, act_sem)
    act_copy.start()

    @pl.loop(1, depth)
    def _(off):
        term_copy(lax.rem(layer + toward * off + depth, depth), off).wait_recv()

    pack(sums.at[spot], *unpack(terms))
    for off in range(1, plane):
        sum_copy(spot, off).start()
    gather.drain()
    for off in range(1, plane):
        sum_copy(lax.rem(spot + off, plane), off).wait_recv()

    weight_sum, bias_sum = unpack(sums)
    grad_scale = float(nodes * n_rows) ** (-0.5)
    finals[replica] = weight_sum * grad_scale

    def final_copy(source, target):
        return pltpu.make_async_remote_copy(
            src_ref=finals.at[source],
            dst_ref=finals.at[source],
            send_sem=final_send.at[target],
            recv_sem=final_recv.at[source],
            device_id=(row, target),
            device_id_type=MESH,
        )

    for off in range(1, replicas):
        final_copy(replica, lax.rem(replica + off, replicas)).start()
    for j in range(replicas):
        bias_out[:, j * col_width:(j + 1) * col_width] = bias_sum[j:j + 1] * grad_scale

    @pl.loop(1, depth)
    def _(off):
        term_copy(layer, off).wait_send()

    for off in range(1, plane):
        sum_copy(spot, off).wait_send()
    for off in range(1, replicas):
        part_copy(replica, lax.rem(replica + off, replicas)).wait_send()
    act_copy.wait()
    for off in range(1, replicas):
        final_copy(lax.rem(replica + replicas - off, replicas), replica).wait_recv()
    for j in range(replicas):
        weight_out[:, j * col_width:(j + 1) * col_width] = finals[j]
    for off in range(1, replicas):
        final_copy(replica, lax.rem(replica + off, replicas)).wait_send()


def publish(act_in, weight_in, bias_in, act_out, weight_out, bias_out, sem):
    copies = [
        pltpu.make_async_copy(source, target, sem.at[k])
        for k, (source, target) in enumerate(
            [(act_in, act_out), (weight_in, weight_out), (bias_in, bias_out)]
        )
    ]
    for copy in copies:
        copy.start()
    for copy in copies:
        copy.wait()


def body(n_rows, replicas, features, node_order, tile_vals, tile_row, tile_col, tile_count, weight, bias, cotangent):
    nodes, feat_width = features.shape
    hid = cotangent.shape[1]
    slots, tile_size, _ = tile_vals.shape
    row_blocks = nodes // tile_size
    half_blocks = row_blocks // replicas
    col_width = hid // replicas
    plane = math.gcd(n_rows, 4)
    depth = n_rows // plane
    chunks = 4
    vmem = pl.BlockSpec(memory_space=pltpu.VMEM)
    dma = pltpu.SemaphoreType.DMA
    tile_total = tile_count.reshape(1, 1)
    activations, weight_grad, bias_grad = pl.pallas_call(
        functools.partial(kernel, n_rows, replicas, plane, chunks, 24),
        out_shape=(
            jax.ShapeDtypeStruct((nodes, hid), jnp.bfloat16),
            jax.ShapeDtypeStruct((feat_width, hid), jnp.float32),
            jax.ShapeDtypeStruct((1, hid), jnp.float32),
        ),
        in_specs=[pl.BlockSpec(memory_space=pltpu.HBM)] * 9,
        out_specs=(pl.BlockSpec(memory_space=pltpu.HBM), vmem, vmem),
        scratch_shapes=[
            pltpu.SMEM(tile_row.shape, jnp.int32),
            pltpu.SMEM(tile_col.shape, jnp.int32),
            pltpu.SMEM((1, 1), jnp.int32),
            pltpu.VMEM((1, nodes), jnp.int32),
            pltpu.VMEM(features.shape, features.dtype),
            pltpu.VMEM(weight.shape, weight.dtype),
            pltpu.VMEM((1, hid), jnp.float32),
            pltpu.VMEM(cotangent.shape, cotangent.dtype),
            pltpu.VMEM((nodes, hid), jnp.bfloat16),
            dma((8,)),
            dma(()),
            pltpu.VMEM((slots, tile_size, tile_size), jnp.bfloat16),
            pltpu.VMEM((n_rows * half_blocks + 1, tile_size, feat_width), jnp.bfloat16),
            pltpu.VMEM((nodes, hid), jnp.float32),
            pltpu.VMEM((replicas, row_blocks, tile_size, feat_width), jnp.float32),
            pltpu.VMEM((depth, feat_width + BIAS_ROWS, col_width), jnp.bfloat16),
            pltpu.VMEM((plane, feat_width + BIAS_ROWS, col_width), jnp.bfloat16),
            pltpu.VMEM((replicas, feat_width, col_width), jnp.float32),
            dma((chunks,)),
            dma((depth,)),
            dma((depth, plane)),
            dma((n_rows,)),
            dma((replicas,)),
            dma((replicas,)),
            dma((depth,)),
            dma((depth,)),
            dma((plane,)),
            dma((plane,)),
            dma((replicas,)),
            dma((replicas,)),
        ],
        compiler_params=pltpu.CompilerParams(
            collective_id=0, has_side_effects=True, vmem_limit_bytes=48 * 1024 * 1024
        ),
    )(*(
        operand if operand is tile_total else pltpu.with_memory_space_constraint(operand, pltpu.HBM)
        for operand in (
            tile_row, tile_col, tile_total, node_order.reshape(1, nodes), features, weight,
            bias.reshape(1, hid), cotangent, tile_vals,
        )
    ))
    activations, weight_grad, bias_grad = pl.pallas_call(
        publish,
        out_shape=tuple(
            jax.ShapeDtypeStruct(part.shape, part.dtype)
            for part in (activations, weight_grad, bias_grad)
        ),
        in_specs=[vmem] * 3,
        out_specs=(pl.BlockSpec(memory_space=pltpu.HBM),) * 3,
        scratch_shapes=[dma((3,))],
        compiler_params=pltpu.CompilerParams(vmem_limit_bytes=1024 * 1024),
    )(activations, weight_grad, bias_grad)
    return activations, weight_grad, bias_grad.reshape(hid)


def solution(mesh):
    return jax.shard_map(
        functools.partial(body, mesh.shape["rows"], mesh.shape["rep"]),
        mesh=mesh,
        in_specs=(
            P("rows", None),
            P("rows"),
            P(("rows", "rep"), None, None),
            P(("rows", "rep")),
            P(("rows", "rep")),
            P(("rows", "rep")),
            P(),
            P(),
            P("rows", None),
        ),
        out_specs=(P("rows", None), P(), P()),
        check_vma=False,
    )
```

```python
import functools
import math

import jax
import jax.numpy as jnp
from jax import lax
from jax.experimental import pallas as pl
from jax.experimental.pallas import tpu as pltpu
from jax.sharding import PartitionSpec as P

MESH = pl.DeviceIdType.MESH
BIAS_ROWS = 16
CONTRACT_ROWS = (((0,), (0,)), ((), ()))


def kernel(
    n_rows, replicas, plane, chunks, unroll,
    tile_row_hbm, tile_col_hbm, tile_count_hbm, order_hbm, features_hbm, weight_hbm, bias_hbm,
    cotangent_hbm, tiles_hbm,
    act_out, weight_out, bias_out,
    tile_row, tile_col, tile_count, order, features, weight, bias, cotangent, activated, input_sem,
    act_sem, tiles, sources, grad_reordered, parts, terms, sums, finals,
    tile_sem, gather_column, gather_plane, gather_recv, part_send, part_recv,
    term_send, term_recv, sum_send, sum_recv, final_send, final_recv,
):
    row = lax.axis_index("rows")
    replica = lax.axis_index("rep")
    slots, tile_size, _ = tiles.shape
    nodes, feat_width = features.shape
    hid = cotangent.shape[1]
    row_blocks = nodes // tile_size
    half_blocks = row_blocks // replicas
    zero_block = n_rows * half_blocks
    col_width = hid // replicas
    per_chunk = slots // chunks
    depth = n_rows // plane
    layer = row // plane
    spot = lax.rem(row, plane)
    toward = 1 - 2 * (layer // ((depth + 1) // 2))

    def column_peer(off):
        return lax.rem(layer + toward * off + depth, depth) * plane + spot

    def plane_peer(off):
        return layer * plane + lax.rem(spot + off, plane)

    inputs = [
        pltpu.make_async_copy(source, target, input_sem.at[k])
        for k, (source, target) in enumerate([
            (order_hbm, order), (features_hbm, features), (cotangent_hbm, cotangent),
            (tile_row_hbm, tile_row), (tile_col_hbm, tile_col), (tile_count_hbm, tile_count),
            (weight_hbm, weight), (bias_hbm, bias),
        ])
    ]
    for copy in inputs:
        copy.start()

    def tile_copy(chunk):
        span = pl.ds(chunk * per_chunk, per_chunk)
        return pltpu.make_async_copy(tiles_hbm.at[span], tiles.at[span], tile_sem.at[chunk])

    for chunk in range(chunks):
        tile_copy(chunk).start()

    barrier = pltpu.get_barrier_semaphore()

    def greet(target, target_rep):
        pl.semaphore_signal(
            barrier, inc=1, device_id=(target, target_rep), device_id_type=MESH
        )

    @pl.loop(1, depth)
    def _(off):
        greet(column_peer(off), replica)

    for off in range(1, plane):
        greet(plane_peer(off), replica)
    for off in range(1, replicas):
        greet(row, lax.rem(replica + off, replicas))

    class Spread:
        def __init__(self, view, column_sem, plane_sem, recv_sem):
            self.view, self.recv_sem = view, recv_sem
            self.column_sem, self.plane_sem = column_sem, plane_sem

        def copy(self, block, target, send_sem):
            return pltpu.make_async_remote_copy(
                src_ref=self.view(block),
                dst_ref=self.view(block),
                send_sem=send_sem,
                recv_sem=self.recv_sem.at[block],
                device_id=(target, replica),
                device_id_type=MESH,
            )

        def along_column(self, off):
            return self.copy(row, column_peer(off), self.column_sem.at[off])

        def through_plane(self, step, off):
            block = row if step is None else column_peer(step)
            step = 0 if step is None else step
            return self.copy(block, plane_peer(off), self.plane_sem.at[step, off])

        def start(self):
            @pl.loop(1, depth)
            def _(off):
                self.along_column(depth - off).start()

            for off in range(1, plane):
                self.through_plane(None, off).start()

        def relay(self):
            @pl.loop(1, depth)
            def _(step):
                self.copy(column_peer(step), row, self.column_sem.at[0]).wait_recv()
                for off in range(1, plane):
                    self.through_plane(step, off).start()

        def finish(self):
            for off in range(1, plane):
                beside = lax.rem(spot + off, plane)

                @pl.loop(0, depth)
                def _(level):
                    self.copy(level * plane + beside, row, self.column_sem.at[0]).wait_recv()

        def drain(self):
            @pl.loop(1, depth)
            def _(off):
                self.along_column(off).wait_send()
                for beside in range(1, plane):
                    self.through_plane(off, beside).wait_send()

            for off in range(1, plane):
                self.through_plane(None, off).wait_send()

    def source_view(block):
        return sources.at[pl.ds(block * half_blocks, half_blocks)]

    gather = Spread(source_view, gather_column, gather_plane, gather_recv)

    inputs[0].wait()
    inputs[1].wait()
    local = order[...] - row * nodes
    place = (lax.broadcasted_iota(jnp.int32, (nodes, nodes), 0) == local).astype(jnp.bfloat16)
    mine = lax.dot_general(
        place, features[...], CONTRACT_ROWS, preferred_element_type=jnp.float32
    ).astype(jnp.bfloat16).reshape(replicas, half_blocks, tile_size, feat_width)
    own = mine[0]
    for which in range(1, replicas):
        own = jnp.where(replica == which, mine[which], own)
    sources[pl.ds(row * half_blocks, half_blocks)] = own
    sources[zero_block] = jnp.zeros((tile_size, feat_width), jnp.bfloat16)

    pl.semaphore_wait(barrier, depth - 1 + plane - 1 + replicas - 1)
    gather.start()

    inputs[2].wait()
    grad_reordered[...] = lax.dot_general(
        place, cotangent[...], CONTRACT_ROWS, preferred_element_type=jnp.float32
    )

    gather.relay()

    for copy in inputs[3:]:
        copy.wait()
    for chunk in range(chunks):
        tile_copy(chunk).wait()

    gather.finish()

    live = tile_count[0, 0]
    first_block = row * row_blocks

    def aggregate(step, acc):
        left, right = [], []
        for sub in range(unroll):
            slot = step * unroll + sub
            col = tile_col[slot]
            position = lax.div(col, row_blocks)
            if half_blocks > 1:
                position = position * half_blocks + lax.rem(col, half_blocks)
            block = jnp.where(slot < live, tile_row[slot] - first_block, row_blocks)
            left.append(tiles[slot])
            right.append(
                jnp.concatenate(
                    [
                        sources[jnp.where(block == which, position, zero_block)]
                        for which in range(row_blocks)
                    ],
                    axis=1,
                )
            )
        return acc + jnp.dot(
            jnp.concatenate(left, axis=1),
            jnp.concatenate(right, axis=0),
            preferred_element_type=jnp.float32,
        )

    acc = lax.fori_loop(
        0, slots // unroll, aggregate, jnp.zeros((tile_size, row_blocks * feat_width), jnp.float32)
    )
    for which in range(row_blocks):
        parts[replica, which] = acc[:, which * feat_width:(which + 1) * feat_width]

    def part_copy(source, target):
        return pltpu.make_async_remote_copy(
            src_ref=parts.at[source],
            dst_ref=parts.at[source],
            send_sem=part_send.at[target],
            recv_sem=part_recv.at[source],
            device_id=(row, target),
            device_id_type=MESH,
        )

    for off in range(1, replicas):
        part_copy(replica, lax.rem(replica + off, replicas)).start()
    for off in range(1, replicas):
        part_copy(lax.rem(replica + replicas - off, replicas), replica).wait_recv()

    total = parts[0]
    for which in range(1, replicas):
        total = total + parts[which]
    hidden = total.reshape(nodes, feat_width).astype(jnp.bfloat16)
    pre_act = jnp.dot(hidden, weight[...], preferred_element_type=jnp.float32) + bias[...]
    sigma = 1.0 / (1.0 + jnp.exp(-pre_act))
    slope = sigma * (1.0 + pre_act * (1.0 - sigma))
    scaled = (grad_reordered[...] * slope).astype(jnp.bfloat16)
    weight_term = lax.dot_general(
        hidden, scaled, CONTRACT_ROWS, preferred_element_type=jnp.float32
    )
    own_term = weight_term[:, :col_width]
    for which in range(1, replicas):
        own_term = jnp.where(
            replica == which, weight_term[:, which * col_width:(which + 1) * col_width], own_term
        )
    bias_term = jnp.sum(scaled.astype(jnp.float32), axis=0, keepdims=True)
    bias_term = jnp.concatenate(
        [bias_term[:, j * col_width:(j + 1) * col_width] for j in range(replicas)], axis=0
    )

    def pack(target, term, bias_part):
        high = bias_part.astype(jnp.bfloat16).astype(jnp.float32)
        pad = jnp.zeros((BIAS_ROWS - 2 * replicas, col_width), jnp.float32)
        target[:feat_width] = term.astype(jnp.bfloat16)
        target[feat_width:] = jnp.concatenate([high, bias_part - high, pad], axis=0).astype(
            jnp.bfloat16
        )

    def unpack(held):
        summed = held[0].astype(jnp.float32)
        for k in range(1, held.shape[0]):
            summed = summed + held[k].astype(jnp.float32)
        low = feat_width + replicas
        return summed[:feat_width], summed[feat_width:low] + summed[low:low + replicas]

    def term_copy(source, off):
        return pltpu.make_async_remote_copy(
            src_ref=terms.at[source],
            dst_ref=terms.at[source],
            send_sem=term_send.at[off],
            recv_sem=term_recv.at[source],
            device_id=(column_peer(off), replica),
            device_id_type=MESH,
        )

    def sum_copy(source, off):
        return pltpu.make_async_remote_copy(
            src_ref=sums.at[source],
            dst_ref=sums.at[source],
            send_sem=sum_send.at[off],
            recv_sem=sum_recv.at[source],
            device_id=(plane_peer(off), replica),
            device_id_type=MESH,
        )

    pack(terms.at[layer], own_term, bias_term)

    @pl.loop(1, depth)
    def _(off):
        term_copy(layer, depth - off).start()

    activated[...] = jnp.dot(
        place, (pre_act * sigma).astype(jnp.bfloat16), preferred_element_type=jnp.float32
    ).astype(jnp.bfloat16)
    act_copy = pltpu.make_async_copy(activated, act_out, act_sem)
    act_copy.start()

    @pl.loop(1, depth)
    def _(off):
        term_copy(lax.rem(layer + toward * off + depth, depth), off).wait_recv()

    pack(sums.at[spot], *unpack(terms))
    for off in range(1, plane):
        sum_copy(spot, off).start()
    gather.drain()
    for off in range(1, plane):
        sum_copy(lax.rem(spot + off, plane), off).wait_recv()

    weight_sum, bias_sum = unpack(sums)
    grad_scale = float(nodes * n_rows) ** (-0.5)
    finals[replica] = weight_sum * grad_scale

    def final_copy(source, target):
        return pltpu.make_async_remote_copy(
            src_ref=finals.at[source],
            dst_ref=finals.at[source],
            send_sem=final_send.at[target],
            recv_sem=final_recv.at[source],
            device_id=(row, target),
            device_id_type=MESH,
        )

    for off in range(1, replicas):
        final_copy(replica, lax.rem(replica + off, replicas)).start()
    for j in range(replicas):
        bias_out[:, j * col_width:(j + 1) * col_width] = bias_sum[j:j + 1] * grad_scale

    @pl.loop(1, depth)
    def _(off):
        term_copy(layer, off).wait_send()

    for off in range(1, plane):
        sum_copy(spot, off).wait_send()
    for off in range(1, replicas):
        part_copy(replica, lax.rem(replica + off, replicas)).wait_send()
    act_copy.wait()
    for off in range(1, replicas):
        final_copy(lax.rem(replica + replicas - off, replicas), replica).wait_recv()
    for j in range(replicas):
        weight_out[:, j * col_width:(j + 1) * col_width] = finals[j]
    for off in range(1, replicas):
        final_copy(replica, lax.rem(replica + off, replicas)).wait_send()


def publish(act_in, weight_in, bias_in, act_out, weight_out, bias_out, sem):
    copies = [
        pltpu.make_async_copy(source, target, sem.at[k])
        for k, (source, target) in enumerate(
            [(act_in, act_out), (weight_in, weight_out), (bias_in, bias_out)]
        )
    ]
    for copy in copies:
        copy.start()
    for copy in copies:
        copy.wait()


def body(n_rows, replicas, features, node_order, tile_vals, tile_row, tile_col, tile_count, weight, bias, cotangent):
    nodes, feat_width = features.shape
    hid = cotangent.shape[1]
    slots, tile_size, _ = tile_vals.shape
    row_blocks = nodes // tile_size
    half_blocks = row_blocks // replicas
    col_width = hid // replicas
    plane = math.gcd(n_rows, 4)
    depth = n_rows // plane
    chunks = 4
    vmem = pl.BlockSpec(memory_space=pltpu.VMEM)
    dma = pltpu.SemaphoreType.DMA
    tile_total = tile_count.reshape(1, 1)
    activations, weight_grad, bias_grad = pl.pallas_call(
        functools.partial(kernel, n_rows, replicas, plane, chunks, 48),
        out_shape=(
            jax.ShapeDtypeStruct((nodes, hid), jnp.bfloat16),
            jax.ShapeDtypeStruct((feat_width, hid), jnp.float32),
            jax.ShapeDtypeStruct((1, hid), jnp.float32),
        ),
        in_specs=[pl.BlockSpec(memory_space=pltpu.HBM)] * 9,
        out_specs=(pl.BlockSpec(memory_space=pltpu.HBM), vmem, vmem),
        scratch_shapes=[
            pltpu.SMEM(tile_row.shape, jnp.int32),
            pltpu.SMEM(tile_col.shape, jnp.int32),
            pltpu.SMEM((1, 1), jnp.int32),
            pltpu.VMEM((1, nodes), jnp.int32),
            pltpu.VMEM(features.shape, features.dtype),
            pltpu.VMEM(weight.shape, weight.dtype),
            pltpu.VMEM((1, hid), jnp.float32),
            pltpu.VMEM(cotangent.shape, cotangent.dtype),
            pltpu.VMEM((nodes, hid), jnp.bfloat16),
            dma((8,)),
            dma(()),
            pltpu.VMEM((slots, tile_size, tile_size), jnp.bfloat16),
            pltpu.VMEM((n_rows * half_blocks + 1, tile_size, feat_width), jnp.bfloat16),
            pltpu.VMEM((nodes, hid), jnp.float32),
            pltpu.VMEM((replicas, row_blocks, tile_size, feat_width), jnp.float32),
            pltpu.VMEM((depth, feat_width + BIAS_ROWS, col_width), jnp.bfloat16),
            pltpu.VMEM((plane, feat_width + BIAS_ROWS, col_width), jnp.bfloat16),
            pltpu.VMEM((replicas, feat_width, col_width), jnp.float32),
            dma((chunks,)),
            dma((depth,)),
            dma((depth, plane)),
            dma((n_rows,)),
            dma((replicas,)),
            dma((replicas,)),
            dma((depth,)),
            dma((depth,)),
            dma((plane,)),
            dma((plane,)),
            dma((replicas,)),
            dma((replicas,)),
        ],
        compiler_params=pltpu.CompilerParams(
            collective_id=0, has_side_effects=True, vmem_limit_bytes=48 * 1024 * 1024
        ),
    )(*(
        operand if operand is tile_total else pltpu.with_memory_space_constraint(operand, pltpu.HBM)
        for operand in (
            tile_row, tile_col, tile_total, node_order.reshape(1, nodes), features, weight,
            bias.reshape(1, hid), cotangent, tile_vals,
        )
    ))
    activations, weight_grad, bias_grad = pl.pallas_call(
        publish,
        out_shape=tuple(
            jax.ShapeDtypeStruct(part.shape, part.dtype)
            for part in (activations, weight_grad, bias_grad)
        ),
        in_specs=[vmem] * 3,
        out_specs=(pl.BlockSpec(memory_space=pltpu.HBM),) * 3,
        scratch_shapes=[dma((3,))],
        compiler_params=pltpu.CompilerParams(vmem_limit_bytes=1024 * 1024),
    )(activations, weight_grad, bias_grad)
    return activations, weight_grad, bias_grad.reshape(hid)


def solution(mesh):
    return jax.shard_map(
        functools.partial(body, mesh.shape["rows"], mesh.shape["rep"]),
        mesh=mesh,
        in_specs=(
            P("rows", None),
            P("rows"),
            P(("rows", "rep"), None, None),
            P(("rows", "rep")),
            P(("rows", "rep")),
            P(("rows", "rep")),
            P(),
            P(),
            P("rows", None),
        ),
        out_specs=(P("rows", None), P(), P()),
        check_vma=False,
    )
```
